32 devices in a mesh: bx: 4 (over x, core), by: 4 (over z), bz: 2 (over y).
Axes of the slice: x: 2, y: 2, z: 4, core: 2. Of those that a mesh axis runs over, the one named last changes fastest.
Arguments:
- density: float32 [32, 512, 512], P('bz', 'bx', 'by'), may hold values from 0 to 1
- colors: float32 [3, 128], replicated, may hold values from 0 to 1
- extinction: float32 [128], replicated, may hold values from 0.001 to 0.06
- march_steps: int32 [4, 4, 2], P('bx', 'by'), may hold values from 1 to 16
- depth_rank: int32 [4, 4, 2], P('bx'), may hold values from 0 to 1, as said below
Outputs:
- image: float32 [5, 512, 512], P(None, ('bx', 'by', 'bz'))
The draws below stay inside these ranges and needn't reach their ends.
Inputs may be any that keep to these rules, and one draw needn't show every extreme that they name: All columns share one view: either depth_rank[i, j, k] = k for every brick, or depth_rank[i, j, k] = 1 - k for every brick.
All inputs are finite; a program needn't handle non-finite values.
Results may differ from the reference program's by a relative error of at most 0.0017.
Values sent between devices are 32-bit elements; how exact they have to be, the bound alone decides.
A program may use at most 64 MiB of HBM per device.

```python
import math
import jax
import jax.numpy as jnp
from jax import lax

TX = 128
TY = 128
BZ = 16
TFN = 128
NX = 512
NY = 512
NZ = 32
N_BX = 4
N_BY = 4
N_BZ = 2


def draw_depth_rank(key, part):
    flag = jax.random.randint(jax.random.fold_in(key, 7), (), 0, 2)
    levels = jnp.arange(N_BZ, dtype=jnp.int32)
    order = jnp.where(flag == 1, N_BZ - 1 - levels, levels).astype(jnp.int32)
    return jnp.broadcast_to(order[None, None, :], (N_BX, N_BY, N_BZ)).astype(jnp.int32)


def touch_ends(result, stream_key, least, largest):
    longest = result.shape.index(max(result.shape))
    spots = []
    for shift in (0, 1):
        where = [jax.random.randint(jax.random.fold_in(stream_key, axis), (), 0, length) for axis, length in enumerate(result.shape)]
        where[longest] = (where[longest] + shift) % result.shape[longest]
        spots.append(tuple(where))
    return result.at[spots[0]].set(least).at[spots[1]].set(largest)


def block_scale(rng, dims, pieces, least, high):
    gain, own = 1.0, jax.random.fold_in(rng, 6)
    for dim, shards_of in pieces:
        steps = jnp.exp(jax.random.uniform(jax.random.fold_in(own, dim), (shards_of,), jnp.float32, least / len(pieces), high / len(pieces)))
        gain = gain * jnp.repeat(steps, dims[dim] // shards_of).reshape([-1 if axis == dim else 1 for axis in range(len(dims))])
    return gain


def setup_inputs(seed: int = 0) -> dict:
    arg_keys = jax.random.split(jax.random.key(seed), 6)
    density = jnp.clip(1.0 * jax.random.uniform(arg_keys[0], (NZ, NX, NY), jnp.float32) ** block_scale(arg_keys[0], (NZ, NX, NY), ((0, 2), (1, 4), (2, 4)), -0.2, 0.2), 0.0, 1.0)
    colors = jnp.clip(jax.random.uniform(arg_keys[1], (3, TFN), jnp.float32, 0.0, 1.0), 0.0, 1.0)
    extinction = jnp.clip(jnp.exp(jax.random.uniform(arg_keys[2], (TFN,), jnp.float32, math.log(0.001), math.log(0.06))), 0.001, 0.06)
    march_steps = touch_ends(jax.random.randint(arg_keys[3], (N_BX, N_BY, N_BZ), 1, BZ + 1), jax.random.fold_in(arg_keys[3], 1), 1, BZ).astype(jnp.int32)
    depth_rank = draw_depth_rank(jax.random.fold_in(arg_keys[5], 71), 0)
    return {"density": density, "colors": colors, "extinction": extinction, "march_steps": march_steps, "depth_rank": depth_rank}


def lookup(table, index, frac):
    return table[..., index] * (1.0 - frac) + table[..., index + 1] * frac


def reference(density, colors, extinction, march_steps, depth_rank):
    total = BZ * N_BZ
    backward = depth_rank[0, 0, 0] != 0
    partials = []
    for layer in range(N_BZ):
        count = jnp.repeat(jnp.repeat(march_steps[:, :, layer], TX, 0), TY, 1)
        rank = jnp.repeat(jnp.repeat(depth_rank[:, :, layer], TX, 0), TY, 1)

        def step(carry, cell):
            color, depth, trans = carry
            inner = jnp.where(backward, BZ - 1 - cell, cell).astype(jnp.int32)
            plane = lax.dynamic_index_in_dim(density, layer * BZ + inner, 0, keepdims=False)
            coord = plane * (TFN - 1)
            index = jnp.clip(jnp.floor(coord).astype(jnp.int32), 0, TFN - 2)
            frac = coord - index.astype(coord.dtype)
            rgb = lookup(colors, index, frac)
            kappa = lookup(extinction, index, frac)
            kappa = jnp.where(cell < count, kappa, jnp.zeros_like(kappa))
            keep = jnp.exp(-kappa)
            weight = trans * (1.0 - keep)
            zpos = ((rank * BZ + cell).astype(plane.dtype) + 0.5) / total
            return (color + weight[None] * rgb, depth + weight * zpos, trans * keep), None

        start = (jnp.zeros((3, NX, NY), jnp.float32), jnp.zeros((NX, NY), jnp.float32), jnp.ones((NX, NY), jnp.float32))
        (color, depth, trans), _ = lax.scan(step, start, jnp.arange(BZ, dtype=jnp.int32))
        partials.append(jnp.concatenate([color, depth[None], trans[None]], 0))
    color = jnp.zeros((3, NX, NY), jnp.float32)
    depth = jnp.zeros((NX, NY), jnp.float32)
    trans = jnp.ones((NX, NY), jnp.float32)
    for order in range(N_BZ):
        chosen = jnp.zeros((5, NX, NY), jnp.float32)
        for layer in range(N_BZ):
            match = jnp.repeat(jnp.repeat(depth_rank[:, :, layer] == order, TX, 0), TY, 1)
            chosen = chosen + jnp.where(match[None], partials[layer], jnp.zeros_like(partials[layer]))
        color = color + trans[None] * chosen[:3]
        depth = depth + trans * chosen[3]
        trans = trans * chosen[4]
    return jnp.concatenate([color, depth[None], (1.0 - trans)[None]], 0)
```

```python
import functools

import jax
import jax.numpy as jnp
from jax import lax
from jax.experimental import pallas as pl
from jax.experimental.pallas import tpu as pltpu
from jax.sharding import PartitionSpec as P

MESH = pl.DeviceIdType.MESH
LOG2E = 1.4426950408889634


def kernel(
    n_by, n_bz,
    density_ref, colors_ref, extinction_ref, steps_ref, ranks_ref,
    out_ref,
    cells_buf, colors_buf, extinction_buf, parts, got, ready,
    load_sem, table_sem, send_z, recv_z, send_y, recv_y,
):
    me_y, me_z = lax.axis_index("by"), lax.axis_index("bz")
    blocks, depth_cells, rows, lanes = cells_buf.shape
    total = depth_cells * n_bz
    points = colors_buf.shape[1]

    others_z = [lax.rem(me_z + o, n_bz) for o in range(1, n_bz)]
    others_y = [lax.rem(me_y + o, n_by) for o in range(1, n_by)]

    barrier = pltpu.get_barrier_semaphore()
    for k in others_z:
        pl.semaphore_signal(barrier, inc=1, device_id={"bz": k}, device_id_type=MESH)
    for j in others_y:
        pl.semaphore_signal(barrier, inc=1, device_id={"by": j}, device_id_type=MESH)

    def table_loads():
        return (
            pltpu.make_async_copy(colors_ref, colors_buf, table_sem.at[0]),
            pltpu.make_async_copy(extinction_ref, extinction_buf, table_sem.at[1]),
        )

    def load(block):
        return pltpu.make_async_copy(density_ref.at[:, block], cells_buf.at[block], load_sem.at[block])

    def target(step):
        return lax.rem(me_y + 1 + step, n_by)

    for copy in table_loads():
        copy.start()
    for o in range(1, n_bz + 1):
        k = lax.rem(me_z + o, n_bz)

        def start(step, carry, k=k):
            load(target(step) * n_bz + k).start()
            return carry

        lax.fori_loop(0, n_by, start, 0)

    rank = ranks_ref[0, me_y, me_z]
    count = steps_ref[0, 0, me_z]
    backward = ranks_ref[0, 0, 0] != 0
    nearest = (rank * depth_cells).astype(jnp.float32) * (1.0 / total)

    for copy in table_loads():
        copy.wait()
    shape = (rows, lanes)

    def pair(row):
        wide = jnp.broadcast_to(row, (8, points))
        slope = pltpu.roll(wide, points - 1, 1) - wide
        return jnp.broadcast_to(wide[:1], (rows, points)), jnp.broadcast_to(slope[:1], (rows, points))

    tables = [pair(colors_buf[c : c + 1]) for c in range(3)] + [pair(extinction_buf[...])]

    def render(block):
        load(block).wait()
        color = [jnp.zeros(shape, jnp.float32) for _ in range(3)]
        depth = jnp.zeros(shape, jnp.float32)
        trans = jnp.ones(shape, jnp.float32)
        for t in range(depth_cells):
            plane = jnp.where(backward, cells_buf[block, depth_cells - 1 - t], cells_buf[block, t])
            coord = plane * (points - 1)
            index = jnp.minimum(coord.astype(jnp.int32), points - 2)
            frac = coord - index.astype(jnp.float32)

            def lookup(table):
                base, slope = (
                    jnp.take_along_axis(half, index, axis=1, mode="promise_in_bounds") for half in table
                )
                return base + frac * slope

            red, green, blue, kappa = [lookup(table) for table in tables]
            keep = jnp.exp2(kappa * jnp.where(t < count, -LOG2E, 0.0))
            weight = trans * (1.0 - keep)
            color = [c + weight * v for c, v in zip(color, (red, green, blue))]
            depth = depth + weight * (nearest + (t + 0.5) / total)
            trans = trans * keep
        return color + [depth, trans]

    def to_layer(block, step, o):
        k = lax.rem(me_z + o, n_bz)
        return pltpu.make_async_remote_copy(
            src_ref=parts.at[block],
            dst_ref=got.at[me_z, step],
            send_sem=send_z.at[block],
            recv_sem=recv_z.at[me_z, step],
            device_id={"bz": k},
            device_id_type=MESH,
        )

    def from_layer(k, step):
        return pltpu.make_async_remote_copy(
            src_ref=parts.at[0],
            dst_ref=got.at[k, step],
            send_sem=send_z.at[0],
            recv_sem=recv_z.at[k, step],
            device_id={"bz": k},
            device_id_type=MESH,
        )

    def columns(j):
        return pl.ds(pl.multiple_of(j * lanes, lanes), lanes)

    def to_owner(step):
        j = target(step)
        return pltpu.make_async_remote_copy(
            src_ref=ready.at[step],
            dst_ref=out_ref.at[:, :, columns(me_y)],
            send_sem=send_y.at[step],
            recv_sem=recv_y.at[me_y],
            device_id={"by": j},
            device_id_type=MESH,
        )

    def from_column(j):
        return pltpu.make_async_remote_copy(
            src_ref=ready.at[0],
            dst_ref=out_ref.at[:, :, columns(j)],
            send_sem=send_y.at[0],
            recv_sem=recv_y.at[j],
            device_id={"by": j},
            device_id_type=MESH,
        )

    def store(ref, slot, values):
        for c, value in enumerate(values):
            ref[slot, c] = value

    def away(step, carry):
        for o in range(1, n_bz):
            block = target(step) * n_bz + lax.rem(me_z + o, n_bz)
            store(parts, block, render(block))

            if o == 1:

                @pl.when(step == 0)
                def _():
                    pl.semaphore_wait(barrier, n_bz - 1 + n_by - 1)

            to_layer(block, step, o).start()
        return carry

    lax.fori_loop(0, n_by, away, 0)

    def merged(step):
        block = target(step) * n_bz + me_z
        for c, value in enumerate(render(block)):
            got[me_z, step, c] = value
        for o in range(1, n_bz):
            from_layer(lax.rem(me_z + o, n_bz), step).wait_recv()
        total_values = None
        for q in range(n_bz):
            layer = [
                jnp.where(backward, got[n_bz - 1 - q, step, c], got[q, step, c]) for c in range(5)
            ]
            if total_values is None:
                total_values = layer
            else:
                through = total_values[4]
                total_values = [a + through * b for a, b in zip(total_values[:4], layer[:4])]
                total_values.append(through * layer[4])
        return total_values[:4] + [1.0 - total_values[4]]

    def own(step, carry):
        store(ready, step, merged(step))
        to_owner(step).start()
        return carry

    lax.fori_loop(0, n_by - 1, own, 0)
    for c, value in enumerate(merged(n_by - 1)):
        out_ref[c, :, columns(me_y)] = value

    for j in others_y:
        from_column(j).wait_recv()

    def finish(step, carry):
        for o in range(1, n_bz):
            to_layer(target(step) * n_bz + lax.rem(me_z + o, n_bz), step, o).wait_send()
        return carry

    lax.fori_loop(0, n_by, finish, 0)

    def finish_owner(step, carry):
        to_owner(step).wait_send()
        return carry

    lax.fori_loop(0, n_by - 1, finish_owner, 0)


def shards(density, colors, extinction, march_steps, depth_rank):
    n_by = lax.axis_size("by")
    n_bz = lax.axis_size("bz")
    depth_cells, tile_x, tile_y = density.shape
    blocks = n_by * n_bz
    rows = tile_x // blocks
    points = colors.shape[1]
    f32 = jnp.float32
    return pl.pallas_call(
        functools.partial(kernel, n_by, n_bz),
        out_shape=jax.ShapeDtypeStruct((5, rows, n_by * tile_y), f32),
        in_specs=[pl.BlockSpec(memory_space=pl.ANY)] * 3 + [pl.BlockSpec(memory_space=pltpu.SMEM)] * 2,
        out_specs=pl.BlockSpec(memory_space=pltpu.VMEM),
        scratch_shapes=[
            pltpu.VMEM((blocks, depth_cells, rows, tile_y), f32),
            pltpu.VMEM((3, points), f32),
            pltpu.VMEM((1, points), f32),
            pltpu.VMEM((blocks, 5, rows, tile_y), f32),
            pltpu.VMEM((n_bz, n_by, 5, rows, tile_y), f32),
            pltpu.VMEM((n_by, 5, rows, tile_y), f32),
            pltpu.SemaphoreType.DMA((blocks,)),
            pltpu.SemaphoreType.DMA((2,)),
            pltpu.SemaphoreType.DMA((blocks,)),
            pltpu.SemaphoreType.DMA((n_bz, n_by)),
            pltpu.SemaphoreType.DMA((n_by,)),
            pltpu.SemaphoreType.DMA((n_by,)),
        ],
        compiler_params=pltpu.CompilerParams(collective_id=0, has_side_effects=True),
    )(
        density.reshape(depth_cells, blocks, rows, tile_y),
        colors,
        extinction.reshape(1, points),
        march_steps,
        depth_rank,
    )


def solution(mesh):
    return jax.shard_map(
        shards,
        mesh=mesh,
        in_specs=(P("bz", "bx", "by"), P(), P(), P("bx", "by", None), P("bx", None, None)),
        out_specs=P(None, ("bx", "by", "bz"), None),
        check_vma=False,
    )
```

```python
import functools

import jax
import jax.numpy as jnp
from jax import lax
from jax.experimental import pallas as pl
from jax.experimental.pallas import tpu as pltpu
from jax.sharding import PartitionSpec as P

MESH = pl.DeviceIdType.MESH
LOG2E = 1.4426950408889634


def kernel(
    n_by, n_bz,
    density_ref, colors_ref, extinction_ref, steps_ref, ranks_ref,
    out_ref,
    cells_buf, colors_buf, extinction_buf, parts, got, ready,
    load_sem, table_sem, send_z, recv_z, send_y, recv_y,
):
    me_y, me_z = lax.axis_index("by"), lax.axis_index("bz")
    blocks, depth_cells, rows, lanes = cells_buf.shape
    total = depth_cells * n_bz
    points = colors_buf.shape[1]

    others_z = [lax.rem(me_z + o, n_bz) for o in range(1, n_bz)]
    others_y = [lax.rem(me_y + o, n_by) for o in range(1, n_by)]

    barrier = pltpu.get_barrier_semaphore()
    for k in others_z:
        pl.semaphore_signal(barrier, inc=1, device_id={"bz": k}, device_id_type=MESH)
    for j in others_y:
        pl.semaphore_signal(barrier, inc=1, device_id={"by": j}, device_id_type=MESH)

    def table_loads():
        return (
            pltpu.make_async_copy(colors_ref, colors_buf, table_sem.at[0]),
            pltpu.make_async_copy(extinction_ref, extinction_buf, table_sem.at[1]),
        )

    def load(block):
        return pltpu.make_async_copy(density_ref.at[:, block], cells_buf.at[block], load_sem.at[block])

    def target(step):
        return lax.rem(me_y + 1 + step, n_by)

    for copy in table_loads():
        copy.start()
    for o in range(1, n_bz + 1):
        k = lax.rem(me_z + o, n_bz)

        def start(step, carry, k=k):
            load(target(step) * n_bz + k).start()
            return carry

        lax.fori_loop(0, n_by, start, 0)

    rank = ranks_ref[0, me_z, me_y]
    count = steps_ref[0, 0, me_z]
    backward = ranks_ref[0, 0, 0] != 0
    nearest = (rank * depth_cells).astype(jnp.float32) * (1.0 / total)

    for copy in table_loads():
        copy.wait()
    shape = (rows, lanes)

    def pair(row):
        wide = jnp.broadcast_to(row, (8, points))
        slope = pltpu.roll(wide, points - 1, 1) - wide
        return jnp.broadcast_to(wide[:1], (rows, points)), jnp.broadcast_to(slope[:1], (rows, points))

    tables = [pair(colors_buf[c : c + 1]) for c in range(3)] + [pair(extinction_buf[...])]

    def render(block):
        load(block).wait()
        color = [jnp.zeros(shape, jnp.float32) for _ in range(3)]
        depth = jnp.zeros(shape, jnp.float32)
        trans = jnp.ones(shape, jnp.float32)
        for t in range(depth_cells):
            plane = jnp.where(backward, cells_buf[block, depth_cells - 1 - t], cells_buf[block, t])
            coord = plane * (points - 1)
            index = jnp.minimum(coord.astype(jnp.int32), points - 2)
            frac = coord - index.astype(jnp.float32)

            def lookup(table):
                base, slope = (
                    jnp.take_along_axis(half, index, axis=1, mode="promise_in_bounds") for half in table
                )
                return base + frac * slope

            red, green, blue, kappa = [lookup(table) for table in tables]
            keep = jnp.exp2(kappa * jnp.where(t < count, -LOG2E, 0.0))
            weight = trans * (1.0 - keep)
            color = [c + weight * v for c, v in zip(color, (red, green, blue))]
            depth = depth + weight * (nearest + (t + 0.5) / total)
            trans = trans * keep
        return color + [depth, trans]

    def to_layer(block, step, o):
        k = lax.rem(me_z + o, n_bz)
        return pltpu.make_async_remote_copy(
            src_ref=parts.at[block],
            dst_ref=got.at[me_z, step],
            send_sem=send_z.at[block],
            recv_sem=recv_z.at[me_z, step],
            device_id={"bz": k},
            device_id_type=MESH,
        )

    def from_layer(k, step):
        return pltpu.make_async_remote_copy(
            src_ref=parts.at[0],
            dst_ref=got.at[k, step],
            send_sem=send_z.at[0],
            recv_sem=recv_z.at[k, step],
            device_id={"bz": k},
            device_id_type=MESH,
        )

    def columns(j):
        return pl.ds(pl.multiple_of(j * lanes, lanes), lanes)

    def to_owner(step):
        j = target(step)
        return pltpu.make_async_remote_copy(
            src_ref=ready.at[step],
            dst_ref=out_ref.at[:, :, columns(me_y)],
            send_sem=send_y.at[step],
            recv_sem=recv_y.at[me_y],
            device_id={"by": j},
            device_id_type=MESH,
        )

    def from_column(j):
        return pltpu.make_async_remote_copy(
            src_ref=ready.at[0],
            dst_ref=out_ref.at[:, :, columns(j)],
            send_sem=send_y.at[0],
            recv_sem=recv_y.at[j],
            device_id={"by": j},
            device_id_type=MESH,
        )

    def store(ref, slot, values):
        for c, value in enumerate(values):
            ref[slot, c] = value

    def away(step, carry):
        for o in range(1, n_bz):
            block = target(step) * n_bz + lax.rem(me_z + o, n_bz)
            store(parts, block, render(block))

            if o == 1:

                @pl.when(step == 0)
                def _():
                    pl.semaphore_wait(barrier, n_bz - 1 + n_by - 1)

            to_layer(block, step, o).start()
        return carry

    lax.fori_loop(0, n_by, away, 0)

    def merged(step):
        block = target(step) * n_bz + me_z
        for c, value in enumerate(render(block)):
            got[me_z, step, c] = value
        for o in range(1, n_bz):
            from_layer(lax.rem(me_z + o, n_bz), step).wait_recv()
        total_values = None
        for q in range(n_bz):
            layer = [
                jnp.where(backward, got[n_bz - 1 - q, step, c], got[q, step, c]) for c in range(5)
            ]
            if total_values is None:
                total_values = layer
            else:
                through = total_values[4]
                total_values = [a + through * b for a, b in zip(total_values[:4], layer[:4])]
                total_values.append(through * layer[4])
        return total_values[:4] + [1.0 - total_values[4]]

    def own(step, carry):
        store(ready, step, merged(step))
        to_owner(step).start()
        return carry

    lax.fori_loop(0, n_by - 1, own, 0)
    for c, value in enumerate(merged(n_by - 1)):
        out_ref[c, :, columns(me_y)] = value

    for j in others_y:
        from_column(j).wait_recv()

    def finish(step, carry):
        for o in range(1, n_bz):
            to_layer(target(step) * n_bz + lax.rem(me_z + o, n_bz), step, o).wait_send()
        return carry

    lax.fori_loop(0, n_by, finish, 0)

    def finish_owner(step, carry):
        to_owner(step).wait_send()
        return carry

    lax.fori_loop(0, n_by - 1, finish_owner, 0)


def shards(density, colors, extinction, march_steps, depth_rank):
    n_by = lax.axis_size("by")
    n_bz = lax.axis_size("bz")
    depth_cells, tile_x, tile_y = density.shape
    blocks = n_by * n_bz
    rows = tile_x // blocks
    points = colors.shape[1]
    f32 = jnp.float32
    return pl.pallas_call(
        functools.partial(kernel, n_by, n_bz),
        out_shape=pltpu.VMEM((5, rows, n_by * tile_y), f32),
        in_specs=[pl.BlockSpec(memory_space=pltpu.HBM)] * 3 + [pl.BlockSpec(memory_space=pltpu.SMEM)] * 2,
        out_specs=pl.BlockSpec(memory_space=pltpu.VMEM),
        scratch_shapes=[
            pltpu.VMEM((blocks, depth_cells, rows, tile_y), f32),
            pltpu.VMEM((3, points), f32),
            pltpu.VMEM((1, points), f32),
            pltpu.VMEM((blocks, 5, rows, tile_y), f32),
            pltpu.VMEM((n_bz, n_by, 5, rows, tile_y), f32),
            pltpu.VMEM((n_by, 5, rows, tile_y), f32),
            pltpu.SemaphoreType.DMA((blocks,)),
            pltpu.SemaphoreType.DMA((2,)),
            pltpu.SemaphoreType.DMA((blocks,)),
            pltpu.SemaphoreType.DMA((n_bz, n_by)),
            pltpu.SemaphoreType.DMA((n_by,)),
            pltpu.SemaphoreType.DMA((n_by,)),
        ],
        compiler_params=pltpu.CompilerParams(collective_id=0, has_side_effects=True),
    )(
        density.reshape(depth_cells, blocks, rows, tile_y),
        colors,
        extinction.reshape(1, points),
        march_steps,
        depth_rank.transpose(0, 2, 1),
    )


def solution(mesh):
    return jax.shard_map(
        shards,
        mesh=mesh,
        in_specs=(P("bz", "bx", "by"), P(), P(), P("bx", "by", None), P("bx", None, None)),
        out_specs=P(None, ("bx", "by", "bz"), None),
        check_vma=False,
    )
```

```python
import functools

import jax
import jax.numpy as jnp
from jax import lax
from jax.experimental import pallas as pl
from jax.experimental.pallas import tpu as pltpu
from jax.sharding import PartitionSpec as P

MESH = pl.DeviceIdType.MESH
LOG2E = 1.4426950408889634
STEPS = 32767
FINE = 65535
SHIFT = 65536
PICK = lax.GatherDimensionNumbers(
    offset_dims=(),
    collapsed_slice_dims=(1,),
    start_index_map=(1,),
    operand_batching_dims=(0,),
    start_indices_batching_dims=(0,),
)


def kernel(
    n_by, n_bz,
    density_ref, colors_ref, extinction_ref, steps_ref, ranks_ref,
    out_ref,
    cells_buf, colors_buf, extinction_buf, parts, got, ready,
    load_sem, table_sem, send_z, recv_z, send_y, recv_y,
):
    me_y, me_z = lax.axis_index("by"), lax.axis_index("bz")
    blocks, depth_cells, rows, lanes = cells_buf.shape
    total = depth_cells * n_bz
    points = colors_buf.shape[1]

    others_z = [lax.rem(me_z + o, n_bz) for o in range(1, n_bz)]
    others_y = [lax.rem(me_y + o, n_by) for o in range(1, n_by)]

    barrier = pltpu.get_barrier_semaphore()
    for k in others_z:
        pl.semaphore_signal(barrier, inc=1, device_id={"bz": k}, device_id_type=MESH)
    for j in others_y:
        pl.semaphore_signal(barrier, inc=1, device_id={"by": j}, device_id_type=MESH)

    def table_loads():
        return (
            pltpu.make_async_copy(colors_ref, colors_buf, table_sem.at[0]),
            pltpu.make_async_copy(extinction_ref, extinction_buf, table_sem.at[1]),
        )

    def load(block):
        return pltpu.make_async_copy(density_ref.at[:, block], cells_buf.at[block], load_sem.at[block])

    def target(step):
        return lax.rem(me_y + 1 + step, n_by)

    for copy in table_loads():
        copy.start()
    for o in range(1, n_bz + 1):
        k = lax.rem(me_z + o, n_bz)

        def start(step, carry, k=k):
            load(target(step) * n_bz + k).start()
            return carry

        lax.fori_loop(0, n_by, start, 0)

    rank = ranks_ref[0, me_z, me_y]
    count = steps_ref[0, 0, me_z]
    backward = ranks_ref[0, 0, 0] != 0
    nearest = (rank * depth_cells).astype(jnp.float32) * (1.0 / total)

    for copy in table_loads():
        copy.wait()

    sub = min(rows, 8)

    def spread(table):
        return jnp.broadcast_to(table[:1], (sub, points))

    def packed(row):
        wide = jnp.broadcast_to(jnp.floor(row * STEPS + 0.5), (8, points)).astype(jnp.int32)
        return spread(wide * SHIFT + (pltpu.roll(wide, points - 1, 1) - wide))

    rgb_tables = [packed(colors_buf[c : c + 1]) for c in range(3)]

    largest = jnp.broadcast_to(jnp.max(extinction_buf[...], axis=1, keepdims=True), (8, points))
    fine = jnp.floor(extinction_buf[...] * (FINE / largest) + 0.5).astype(jnp.int32)
    kappa_tables = [spread(fine * SHIFT + pltpu.roll(fine, points - 1, 1))]
    scale = spread(largest * (-LOG2E / FINE))

    def look_up(block, t, part):
        at = pl.ds(part * sub, sub)
        plane = jnp.where(backward, cells_buf[block, depth_cells - 1 - t, at], cells_buf[block, t, at])
        coord = plane * (points - 1)
        index = coord.astype(jnp.int32)
        frac = coord - index.astype(jnp.float32)
        tilt = frac * SHIFT - 1.0

        def pick(table):
            return lax.gather(
                table, index[..., None], PICK, (1, 1), mode=lax.GatherScatterMode.PROMISE_IN_BOUNDS
            )

        picked = [pick(table) for table in rgb_tables + kappa_tables]
        rgb = []
        for both in picked[:3]:
            step = lax.shift_right_arithmetic(lax.shift_left(both, 16), 16)
            rgb.append(both.astype(jnp.float32) + step.astype(jnp.float32) * tilt)
        base = lax.shift_right_logical(picked[3], 16).astype(jnp.float32)
        kappa = base + frac * ((picked[3] & 65535).astype(jnp.float32) - base)
        return rgb, kappa

    def render(block):
        load(block).wait()
        shape = (sub, lanes)
        parts_of = []
        for part in range(rows // sub):
            parts_of.append([jnp.zeros(shape, jnp.float32)] * 4 + [jnp.ones(shape, jnp.float32)])
        for t in range(depth_cells):
            absorb = jnp.where(t < count, scale, 0.0)
            position = nearest + (t + 0.5) / total
            for part, (red, green, blue, depth, trans) in enumerate(parts_of):
                rgb, kappa = look_up(block, t, part)
                keep = jnp.exp2(kappa * absorb)
                weight = trans * (1.0 - keep)
                color = [c + weight * v for c, v in zip((red, green, blue), rgb)]
                parts_of[part] = color + [depth + weight * position, trans * keep]
        return [[c * (1.0 / (SHIFT * STEPS)) for c in p[:3]] + p[3:] for p in parts_of]

    def to_layer(block, step, o):
        k = lax.rem(me_z + o, n_bz)
        return pltpu.make_async_remote_copy(
            src_ref=parts.at[block],
            dst_ref=got.at[me_z, step],
            send_sem=send_z.at[block],
            recv_sem=recv_z.at[me_z, step],
            device_id={"bz": k},
            device_id_type=MESH,
        )

    def from_layer(k, step):
        return pltpu.make_async_remote_copy(
            src_ref=parts.at[0],
            dst_ref=got.at[k, step],
            send_sem=send_z.at[0],
            recv_sem=recv_z.at[k, step],
            device_id={"bz": k},
            device_id_type=MESH,
        )

    def columns(j):
        return pl.ds(pl.multiple_of(j * lanes, lanes), lanes)

    def to_owner(step):
        j = target(step)
        return pltpu.make_async_remote_copy(
            src_ref=ready.at[step],
            dst_ref=out_ref.at[:, :, columns(me_y)],
            send_sem=send_y.at[step],
            recv_sem=recv_y.at[me_y],
            device_id={"by": j},
            device_id_type=MESH,
        )

    def from_column(j):
        return pltpu.make_async_remote_copy(
            src_ref=ready.at[0],
            dst_ref=out_ref.at[:, :, columns(j)],
            send_sem=send_y.at[0],
            recv_sem=recv_y.at[j],
            device_id={"by": j},
            device_id_type=MESH,
        )

    def store(ref, slot, values):
        for part, channels in enumerate(values):
            for c, value in enumerate(channels):
                ref[(*slot, c, pl.ds(part * sub, sub))] = value

    def away(step, carry):
        for o in range(1, n_bz):
            block = target(step) * n_bz + lax.rem(me_z + o, n_bz)
            store(parts, (block,), render(block))

            if o == 1:

                @pl.when(step == 0)
                def _():
                    pl.semaphore_wait(barrier, n_bz - 1 + n_by - 1)

            to_layer(block, step, o).start()
        return carry

    lax.fori_loop(0, n_by, away, 0)

    def merged(step):
        block = target(step) * n_bz + me_z
        store(got, (me_z, step), render(block))
        for o in range(1, n_bz):
            from_layer(lax.rem(me_z + o, n_bz), step).wait_recv()
        total_values = None
        for q in range(n_bz):
            layer = [
                jnp.where(backward, got[n_bz - 1 - q, step, c], got[q, step, c]) for c in range(5)
            ]
            if total_values is None:
                total_values = layer
            else:
                through = total_values[4]
                total_values = [a + through * b for a, b in zip(total_values[:4], layer[:4])]
                total_values.append(through * layer[4])
        return total_values[:4] + [1.0 - total_values[4]]

    def own(step, carry):
        for c, value in enumerate(merged(step)):
            ready[step, c] = value

        to_owner(step).start()
        return carry

    lax.fori_loop(0, n_by - 1, own, 0)
    for c, value in enumerate(merged(n_by - 1)):
        out_ref[c, :, columns(me_y)] = value

    for j in others_y:
        from_column(j).wait_recv()

    def finish(step, carry):
        for o in range(1, n_bz):
            to_layer(target(step) * n_bz + lax.rem(me_z + o, n_bz), step, o).wait_send()
        return carry

    lax.fori_loop(0, n_by, finish, 0)

    def finish_owner(step, carry):
        to_owner(step).wait_send()
        return carry

    lax.fori_loop(0, n_by - 1, finish_owner, 0)


def shards(density, colors, extinction, march_steps, depth_rank):
    n_by = lax.axis_size("by")
    n_bz = lax.axis_size("bz")
    depth_cells, tile_x, tile_y = density.shape
    blocks = n_by * n_bz
    rows = tile_x // blocks
    points = colors.shape[1]
    f32 = jnp.float32
    return pl.pallas_call(
        functools.partial(kernel, n_by, n_bz),
        out_shape=pltpu.VMEM((5, rows, n_by * tile_y), f32),
        in_specs=[pl.BlockSpec(memory_space=pltpu.HBM)] * 3 + [pl.BlockSpec(memory_space=pltpu.SMEM)] * 2,
        out_specs=pl.BlockSpec(memory_space=pltpu.VMEM),
        scratch_shapes=[
            pltpu.VMEM((blocks, depth_cells, rows, tile_y), f32),
            pltpu.VMEM((3, points), f32),
            pltpu.VMEM((1, points), f32),
            pltpu.VMEM((blocks, 5, rows, tile_y), f32),
            pltpu.VMEM((n_bz, n_by, 5, rows, tile_y), f32),
            pltpu.VMEM((n_by, 5, rows, tile_y), f32),
            pltpu.SemaphoreType.DMA((blocks,)),
            pltpu.SemaphoreType.DMA((2,)),
            pltpu.SemaphoreType.DMA((blocks,)),
            pltpu.SemaphoreType.DMA((n_bz, n_by)),
            pltpu.SemaphoreType.DMA((n_by,)),
            pltpu.SemaphoreType.DMA((n_by,)),
        ],
        compiler_params=pltpu.CompilerParams(collective_id=0, has_side_effects=True),
    )(
        density.reshape(depth_cells, blocks, rows, tile_y),
        colors,
        extinction.reshape(1, points),
        march_steps,
        depth_rank.transpose(0, 2, 1),
    )


def solution(mesh):
    return jax.shard_map(
        shards,
        mesh=mesh,
        in_specs=(P("bz", "bx", "by"), P(), P(), P("bx", "by", None), P("bx", None, None)),
        out_specs=P(None, ("bx", "by", "bz"), None),
        check_vma=False,
    )
```

```python
import functools

import jax
import jax.numpy as jnp
from jax import lax
from jax.experimental import pallas as pl
from jax.experimental.pallas import tpu as pltpu
from jax.sharding import PartitionSpec as P

MESH = pl.DeviceIdType.MESH
LOG2E = 1.4426950408889634
STEPS = 32767
FINE = 65535
SHIFT = 65536
PICK = lax.GatherDimensionNumbers(
    offset_dims=(),
    collapsed_slice_dims=(1,),
    start_index_map=(1,),
    operand_batching_dims=(0,),
    start_indices_batching_dims=(0,),
)


def kernel(
    n_by, n_bz,
    density_ref, colors_ref, extinction_ref, steps_hbm, ranks_hbm,
    out_ref,
    cells_buf, colors_buf, extinction_buf, steps_ref, ranks_ref, parts, got, ready,
    load_sem, table_sem, send_z, recv_z, send_y, recv_y,
):
    me_y, me_z = lax.axis_index("by"), lax.axis_index("bz")
    blocks, depth_cells, rows, lanes = cells_buf.shape
    total = depth_cells * n_bz
    points = colors_buf.shape[1]

    others_z = [lax.rem(me_z + o, n_bz) for o in range(1, n_bz)]
    others_y = [lax.rem(me_y + o, n_by) for o in range(1, n_by)]

    barrier = pltpu.get_barrier_semaphore()
    for k in others_z:
        pl.semaphore_signal(barrier, inc=1, device_id={"bz": k}, device_id_type=MESH)
    for j in others_y:
        pl.semaphore_signal(barrier, inc=1, device_id={"by": j}, device_id_type=MESH)

    def table_loads():
        return (
            pltpu.make_async_copy(colors_ref, colors_buf, table_sem.at[0]),
            pltpu.make_async_copy(extinction_ref, extinction_buf, table_sem.at[1]),
            pltpu.make_async_copy(steps_hbm, steps_ref, table_sem.at[2]),
            pltpu.make_async_copy(ranks_hbm, ranks_ref, table_sem.at[3]),
        )

    def load(block):
        return pltpu.make_async_copy(density_ref.at[:, block], cells_buf.at[block], load_sem.at[block])

    def target(step):
        if n_by & (n_by - 1):
            return lax.rem(me_y + 1 + step, n_by)
        flips, column, weight = n_by - 1 - step, 0, 1
        while weight < n_by:
            column = column + weight * lax.rem(me_y // weight + flips // weight, 2)
            weight *= 2
        return column

    for copy in table_loads():
        copy.start()
    for o in range(1, n_bz + 1):
        k = lax.rem(me_z + o, n_bz)

        def start(step, carry, k=k):
            load(target(step) * n_bz + k).start()
            return carry

        lax.fori_loop(0, n_by, start, 0)

    for copy in table_loads():
        copy.wait()
    rank = ranks_ref[0, me_z, me_y]
    count = steps_ref[0, 0, me_z]
    backward = ranks_ref[0, 0, 0] != 0
    nearest = (rank * depth_cells).astype(jnp.float32) * (1.0 / total)

    sub = min(rows, 8)

    def spread(table):
        return jnp.broadcast_to(table[:1], (sub, points))

    def packed(row):
        wide = jnp.broadcast_to(jnp.floor(row * STEPS + 0.5), (8, points)).astype(jnp.int32)
        return spread(wide * SHIFT + (pltpu.roll(wide, points - 1, 1) - wide))

    rgb_tables = [packed(colors_buf[c : c + 1]) for c in range(3)]

    largest = jnp.broadcast_to(jnp.max(extinction_buf[...], axis=1, keepdims=True), (8, points))
    fine = jnp.floor(extinction_buf[...] * (FINE / largest) + 0.5).astype(jnp.int32)
    kappa_tables = [spread(fine * SHIFT + pltpu.roll(fine, points - 1, 1))]
    scale = spread(largest * (-LOG2E / FINE))

    def look_up(block, t, part):
        at = pl.ds(part * sub, sub)
        plane = jnp.where(backward, cells_buf[block, depth_cells - 1 - t, at], cells_buf[block, t, at])
        coord = plane * (points - 1)
        index = coord.astype(jnp.int32)
        frac = coord - index.astype(jnp.float32)
        tilt = frac * SHIFT - 1.0

        def pick(table):
            return lax.gather(
                table, index[..., None], PICK, (1, 1), mode=lax.GatherScatterMode.PROMISE_IN_BOUNDS
            )

        picked = [pick(table) for table in rgb_tables + kappa_tables]
        rgb = []
        for both in picked[:3]:
            step = lax.shift_right_arithmetic(lax.shift_left(both, 16), 16)
            rgb.append(both.astype(jnp.float32) + step.astype(jnp.float32) * tilt)
        base = lax.shift_right_logical(picked[3], 16).astype(jnp.float32)
        kappa = base + frac * ((picked[3] & 65535).astype(jnp.float32) - base)
        return rgb, kappa

    def render(block):
        load(block).wait()
        shape = (sub, lanes)
        parts_of = []
        for part in range(rows // sub):
            parts_of.append([jnp.zeros(shape, jnp.float32)] * 4 + [jnp.ones(shape, jnp.float32)])
        for t in range(depth_cells):
            absorb = jnp.where(t < count, scale, 0.0)
            position = nearest + (t + 0.5) / total
            for part, (red, green, blue, depth, trans) in enumerate(parts_of):
                rgb, kappa = look_up(block, t, part)
                keep = jnp.exp2(kappa * absorb)
                weight = trans * (1.0 - keep)
                color = [c + weight * v for c, v in zip((red, green, blue), rgb)]
                parts_of[part] = color + [depth + weight * position, trans * keep]
        return [[c * (1.0 / (SHIFT * STEPS)) for c in p[:3]] + p[3:] for p in parts_of]

    def to_layer(block, step, o):
        k = lax.rem(me_z + o, n_bz)
        return pltpu.make_async_remote_copy(
            src_ref=parts.at[block],
            dst_ref=got.at[me_z, step],
            send_sem=send_z.at[block],
            recv_sem=recv_z.at[me_z, step],
            device_id={"bz": k},
            device_id_type=MESH,
        )

    def from_layer(k, step):
        return pltpu.make_async_remote_copy(
            src_ref=parts.at[0],
            dst_ref=got.at[k, step],
            send_sem=send_z.at[0],
            recv_sem=recv_z.at[k, step],
            device_id={"bz": k},
            device_id_type=MESH,
        )

    def columns(j):
        return pl.ds(pl.multiple_of(j * lanes, lanes), lanes)

    def to_owner(step):
        j = target(step)
        return pltpu.make_async_remote_copy(
            src_ref=ready.at[step],
            dst_ref=out_ref.at[:, :, columns(me_y)],
            send_sem=send_y.at[step],
            recv_sem=recv_y.at[me_y],
            device_id={"by": j},
            device_id_type=MESH,
        )

    def from_column(j):
        return pltpu.make_async_remote_copy(
            src_ref=ready.at[0],
            dst_ref=out_ref.at[:, :, columns(j)],
            send_sem=send_y.at[0],
            recv_sem=recv_y.at[j],
            device_id={"by": j},
            device_id_type=MESH,
        )

    def store(ref, slot, values):
        for part, channels in enumerate(values):
            for c, value in enumerate(channels):
                ref[(*slot, c, pl.ds(part * sub, sub))] = value

    def away(step, carry):
        for o in range(1, n_bz):
            block = target(step) * n_bz + lax.rem(me_z + o, n_bz)
            store(parts, (block,), render(block))

            if o == 1:

                @pl.when(step == 0)
                def _():
                    pl.semaphore_wait(barrier, n_bz - 1 + n_by - 1)

            to_layer(block, step, o).start()
        return carry

    lax.fori_loop(0, n_by, away, 0)

    def merged(step):
        block = target(step) * n_bz + me_z
        store(got, (me_z, step), render(block))
        for o in range(1, n_bz):
            from_layer(lax.rem(me_z + o, n_bz), step).wait_recv()
        total_values = None
        for q in range(n_bz):
            layer = [
                jnp.where(backward, got[n_bz - 1 - q, step, c], got[q, step, c]) for c in range(5)
            ]
            if total_values is None:
                total_values = layer
            else:
                through = total_values[4]
                total_values = [a + through * b for a, b in zip(total_values[:4], layer[:4])]
                total_values.append(through * layer[4])
        return total_values[:4] + [1.0 - total_values[4]]

    def own(step, carry):
        for c, value in enumerate(merged(step)):
            ready[step, c] = value

        to_owner(step).start()
        return carry

    lax.fori_loop(0, n_by - 1, own, 0)
    for c, value in enumerate(merged(n_by - 1)):
        out_ref[c, :, columns(me_y)] = value

    for j in others_y:
        from_column(j).wait_recv()

    def finish(step, carry):
        for o in range(1, n_bz):
            to_layer(target(step) * n_bz + lax.rem(me_z + o, n_bz), step, o).wait_send()
        return carry

    lax.fori_loop(0, n_by, finish, 0)

    def finish_owner(step, carry):
        to_owner(step).wait_send()
        return carry

    lax.fori_loop(0, n_by - 1, finish_owner, 0)


def shards(density, colors, extinction, march_steps, depth_rank):
    n_by = lax.axis_size("by")
    n_bz = lax.axis_size("bz")
    depth_cells, tile_x, tile_y = density.shape
    blocks = n_by * n_bz
    rows = tile_x // blocks
    points = colors.shape[1]
    f32 = jnp.float32
    return pl.pallas_call(
        functools.partial(kernel, n_by, n_bz),
        out_shape=pltpu.VMEM((5, rows, n_by * tile_y), f32),
        in_specs=[pl.BlockSpec(memory_space=pl.ANY)] * 5,
        out_specs=pl.BlockSpec(memory_space=pltpu.VMEM),
        scratch_shapes=[
            pltpu.VMEM((blocks, depth_cells, rows, tile_y), f32),
            pltpu.VMEM((3, points), f32),
            pltpu.VMEM((1, points), f32),
            pltpu.SMEM(march_steps.shape, jnp.int32),
            pltpu.SMEM((depth_rank.shape[0], depth_rank.shape[2], depth_rank.shape[1]), jnp.int32),
            pltpu.VMEM((blocks, 5, rows, tile_y), f32),
            pltpu.VMEM((n_bz, n_by, 5, rows, tile_y), f32),
            pltpu.VMEM((n_by, 5, rows, tile_y), f32),
            pltpu.SemaphoreType.DMA((blocks,)),
            pltpu.SemaphoreType.DMA((4,)),
            pltpu.SemaphoreType.DMA((blocks,)),
            pltpu.SemaphoreType.DMA((n_bz, n_by)),
            pltpu.SemaphoreType.DMA((n_by,)),
            pltpu.SemaphoreType.DMA((n_by,)),
        ],
        compiler_params=pltpu.CompilerParams(collective_id=0, has_side_effects=True),
    )(
        density.reshape(depth_cells, blocks, rows, tile_y),
        colors,
        extinction.reshape(1, points),
        march_steps,
        depth_rank.transpose(0, 2, 1),
    )


def solution(mesh):
    return jax.shard_map(
        shards,
        mesh=mesh,
        in_specs=(P("bz", "bx", "by"), P(), P(), P("bx", "by", None), P("bx", None, None)),
        out_specs=P(None, ("bx", "by", "bz"), None),
        check_vma=False,
    )
```

```python
import functools

import jax
import jax.numpy as jnp
from jax import lax
from jax.experimental import pallas as pl
from jax.experimental.pallas import tpu as pltpu
from jax.sharding import PartitionSpec as P

MESH = pl.DeviceIdType.MESH
LOG2E = 1.4426950408889634
STEPS = 32767
FINE = 65535
SHIFT = 65536
PICK = lax.GatherDimensionNumbers(
    offset_dims=(),
    collapsed_slice_dims=(1,),
    start_index_map=(1,),
    operand_batching_dims=(0,),
    start_indices_batching_dims=(0,),
)


def kernel(
    n_by, n_bz,
    density_ref, colors_ref, extinction_ref, steps_hbm, ranks_hbm,
    out_ref,
    cells_buf, colors_buf, extinction_buf, steps_ref, ranks_ref, parts, got, ready,
    load_sem, table_sem, send_z, recv_z, send_y, recv_y,
):
    me_y, me_z = lax.axis_index("by"), lax.axis_index("bz")
    blocks, depth_cells, rows, lanes = cells_buf.shape
    pieces = out_ref.shape[1] // rows
    total = depth_cells * n_bz
    points = colors_buf.shape[1]

    others_z = [lax.rem(me_z + o, n_bz) for o in range(1, n_bz)]
    others_y = [lax.rem(me_y + o, n_by) for o in range(1, n_by)]

    barrier = pltpu.get_barrier_semaphore()
    for k in others_z:
        pl.semaphore_signal(barrier, inc=1, device_id={"bz": k}, device_id_type=MESH)
    for j in others_y:
        pl.semaphore_signal(barrier, inc=1, device_id={"by": j}, device_id_type=MESH)

    def table_loads():
        return (
            pltpu.make_async_copy(colors_ref, colors_buf, table_sem.at[0]),
            pltpu.make_async_copy(extinction_ref, extinction_buf, table_sem.at[1]),
            pltpu.make_async_copy(steps_hbm, steps_ref, table_sem.at[2]),
            pltpu.make_async_copy(ranks_hbm, ranks_ref, table_sem.at[3]),
        )

    def load(block):
        return pltpu.make_async_copy(density_ref.at[:, block], cells_buf.at[block], load_sem.at[block])

    def target(step):
        if n_by & (n_by - 1):
            return lax.rem(me_y + 1 + step // pieces, n_by)
        flips, column, weight = n_by - 1 - step // pieces, 0, 1
        while weight < n_by:
            column = column + weight * lax.rem(me_y // weight + flips // weight, 2)
            weight *= 2
        return column

    def block_of(step, k):
        return (target(step) * n_bz + k) * pieces + lax.rem(step, pieces)

    for copy in table_loads():
        copy.start()
    for o in range(1, n_bz + 1):
        k = lax.rem(me_z + o, n_bz)

        def start(step, carry, k=k):
            load(block_of(step, k)).start()
            return carry

        lax.fori_loop(0, n_by * pieces, start, 0)

    for copy in table_loads():
        copy.wait()
    rank = ranks_ref[0, me_z, me_y]
    count = steps_ref[0, 0, me_z]
    backward = ranks_ref[0, 0, 0] != 0
    nearest = (rank * depth_cells).astype(jnp.float32) * (1.0 / total)

    sub = min(rows, 8)

    def spread(table):
        return jnp.broadcast_to(table[:1], (sub, points))

    def packed(row):
        wide = jnp.broadcast_to(jnp.floor(row * STEPS + 0.5), (8, points)).astype(jnp.int32)
        return spread(wide * SHIFT + (pltpu.roll(wide, points - 1, 1) - wide))

    rgb_tables = [packed(colors_buf[c : c + 1]) for c in range(3)]

    largest = jnp.broadcast_to(jnp.max(extinction_buf[...], axis=1, keepdims=True), (8, points))
    fine = jnp.floor(extinction_buf[...] * (FINE / largest) + 0.5).astype(jnp.int32)
    kappa_tables = [spread(fine * SHIFT + pltpu.roll(fine, points - 1, 1))]
    scale = spread(largest * (-LOG2E / FINE))

    def look_up(block, t, part):
        at = pl.ds(part * sub, sub)
        plane = jnp.where(backward, cells_buf[block, depth_cells - 1 - t, at], cells_buf[block, t, at])
        coord = plane * (points - 1)
        index = coord.astype(jnp.int32)
        frac = coord - index.astype(jnp.float32)
        tilt = frac * SHIFT - 1.0

        def pick(table):
            return lax.gather(
                table, index[..., None], PICK, (1, 1), mode=lax.GatherScatterMode.PROMISE_IN_BOUNDS
            )

        picked = [pick(table) for table in rgb_tables + kappa_tables]
        rgb = []
        for both in picked[:3]:
            step = lax.shift_right_arithmetic(lax.shift_left(both, 16), 16)
            rgb.append(both.astype(jnp.float32) + step.astype(jnp.float32) * tilt)
        base = lax.shift_right_logical(picked[3], 16).astype(jnp.float32)
        kappa = base + frac * ((picked[3] & 65535).astype(jnp.float32) - base)
        return rgb, kappa

    def render(block):
        load(block).wait()
        shape = (sub, lanes)
        parts_of = []
        for part in range(rows // sub):
            parts_of.append([jnp.zeros(shape, jnp.float32)] * 4 + [jnp.ones(shape, jnp.float32)])
        for t in range(depth_cells):
            absorb = jnp.where(t < count, scale, 0.0)
            position = nearest + (t + 0.5) / total
            for part, (red, green, blue, depth, trans) in enumerate(parts_of):
                rgb, kappa = look_up(block, t, part)
                keep = jnp.exp2(kappa * absorb)
                weight = trans * (1.0 - keep)
                color = [c + weight * v for c, v in zip((red, green, blue), rgb)]
                parts_of[part] = color + [depth + weight * position, trans * keep]
        return [[c * (1.0 / (SHIFT * STEPS)) for c in p[:3]] + p[3:] for p in parts_of]

    def to_layer(block, step, o):
        k = lax.rem(me_z + o, n_bz)
        return pltpu.make_async_remote_copy(
            src_ref=parts.at[block],
            dst_ref=got.at[me_z, step],
            send_sem=send_z.at[block],
            recv_sem=recv_z.at[me_z, step],
            device_id={"bz": k},
            device_id_type=MESH,
        )

    def from_layer(k, step):
        return pltpu.make_async_remote_copy(
            src_ref=parts.at[0],
            dst_ref=got.at[k, step],
            send_sem=send_z.at[0],
            recv_sem=recv_z.at[k, step],
            device_id={"bz": k},
            device_id_type=MESH,
        )

    def place(j, piece):
        at = pl.multiple_of(piece * rows, rows)
        return out_ref.at[:, pl.ds(at, rows), columns(j)]

    def columns(j):
        return pl.ds(pl.multiple_of(j * lanes, lanes), lanes)

    def to_owner(step):
        piece = lax.rem(step, pieces)
        return pltpu.make_async_remote_copy(
            src_ref=ready.at[step],
            dst_ref=place(me_y, piece),
            send_sem=send_y.at[step],
            recv_sem=recv_y.at[me_y * pieces + piece],
            device_id={"by": target(step)},
            device_id_type=MESH,
        )

    def from_column(j, piece):
        return pltpu.make_async_remote_copy(
            src_ref=ready.at[0],
            dst_ref=place(j, piece),
            send_sem=send_y.at[0],
            recv_sem=recv_y.at[j * pieces + piece],
            device_id={"by": j},
            device_id_type=MESH,
        )

    def store(ref, slot, values):
        for part, channels in enumerate(values):
            for c, value in enumerate(channels):
                ref[(*slot, c, pl.ds(part * sub, sub))] = value

    def away(step, carry):
        for o in range(1, n_bz):
            block = block_of(step, lax.rem(me_z + o, n_bz))
            store(parts, (block,), render(block))

            if o == 1:

                @pl.when(step == 0)
                def _():
                    pl.semaphore_wait(barrier, n_bz - 1 + n_by - 1)

            to_layer(block, step, o).start()
        return carry

    lax.fori_loop(0, n_by * pieces, away, 0)

    def merged(step):
        block = block_of(step, me_z)
        store(got, (me_z, step), render(block))
        for o in range(1, n_bz):
            from_layer(lax.rem(me_z + o, n_bz), step).wait_recv()
        total_values = None
        for q in range(n_bz):
            layer = [
                jnp.where(backward, got[n_bz - 1 - q, step, c], got[q, step, c]) for c in range(5)
            ]
            if total_values is None:
                total_values = layer
            else:
                through = total_values[4]
                total_values = [a + through * b for a, b in zip(total_values[:4], layer[:4])]
                total_values.append(through * layer[4])
        return total_values[:4] + [1.0 - total_values[4]]

    def own(step, carry):
        for c, value in enumerate(merged(step)):
            ready[step, c] = value

        to_owner(step).start()
        return carry

    lax.fori_loop(0, (n_by - 1) * pieces, own, 0)
    for piece in range(pieces):
        for c, value in enumerate(merged((n_by - 1) * pieces + piece)):
            out_ref[c, pl.ds(piece * rows, rows), columns(me_y)] = value

    for j in others_y:
        for piece in range(pieces):
            from_column(j, piece).wait_recv()

    def finish(step, carry):
        for o in range(1, n_bz):
            to_layer(block_of(step, lax.rem(me_z + o, n_bz)), step, o).wait_send()
        return carry

    lax.fori_loop(0, n_by * pieces, finish, 0)

    def finish_owner(step, carry):
        to_owner(step).wait_send()
        return carry

    lax.fori_loop(0, (n_by - 1) * pieces, finish_owner, 0)


def shards(density, colors, extinction, march_steps, depth_rank):
    n_by = lax.axis_size("by")
    n_bz = lax.axis_size("bz")
    depth_cells, tile_x, tile_y = density.shape
    owned = tile_x // (n_by * n_bz)
    rows = owned if owned % 8 else 8
    steps = n_by * (owned // rows)
    blocks = n_bz * steps
    points = colors.shape[1]
    f32 = jnp.float32
    return pl.pallas_call(
        functools.partial(kernel, n_by, n_bz),
        out_shape=pltpu.VMEM((5, owned, n_by * tile_y), f32),
        in_specs=[pl.BlockSpec(memory_space=pl.ANY)] * 5,
        out_specs=pl.BlockSpec(memory_space=pltpu.VMEM),
        scratch_shapes=[
            pltpu.VMEM((blocks, depth_cells, rows, tile_y), f32),
            pltpu.VMEM((3, points), f32),
            pltpu.VMEM((1, points), f32),
            pltpu.SMEM(march_steps.shape, jnp.int32),
            pltpu.SMEM((depth_rank.shape[0], depth_rank.shape[2], depth_rank.shape[1]), jnp.int32),
            pltpu.VMEM((blocks, 5, rows, tile_y), f32),
            pltpu.VMEM((n_bz, steps, 5, rows, tile_y), f32),
            pltpu.VMEM((steps, 5, rows, tile_y), f32),
            pltpu.SemaphoreType.DMA((blocks,)),
            pltpu.SemaphoreType.DMA((4,)),
            pltpu.SemaphoreType.DMA((blocks,)),
            pltpu.SemaphoreType.DMA((n_bz, steps)),
            pltpu.SemaphoreType.DMA((steps,)),
            pltpu.SemaphoreType.DMA((steps,)),
        ],
        compiler_params=pltpu.CompilerParams(collective_id=0, has_side_effects=True),
    )(
        density.reshape(depth_cells, blocks, rows, tile_y),
        colors,
        extinction.reshape(1, points),
        march_steps,
        depth_rank.transpose(0, 2, 1),
    )


def solution(mesh):
    return jax.shard_map(
        shards,
        mesh=mesh,
        in_specs=(P("bz", "bx", "by"), P(), P(), P("bx", "by", None), P("bx", None, None)),
        out_specs=P(None, ("bx", "by", "bz"), None),
        check_vma=False,
    )
```
